32 devices in a mesh: grating: 2 (over x), layer: 4 (over z), harm: 4 (over y, core).
Axes of the slice: x: 2, y: 2, z: 4, core: 2. Of those that a mesh axis runs over, the one named last changes fastest.
Arguments:
- panels: float32 [8, 1280, 2, 640], P(('grating', 'layer'), 'harm'), parts along dimension 0, may hold values from -6 to 6
- factors: float32 [16, 1280, 2, 1280], P(('grating', 'layer'), 'harm'), parts along dimension 0, may hold values from -0.25 to 0.25
- decay: float32 [16, 1280], P(('grating', 'layer'), 'harm'), parts along dimension 0, may hold values from 0.25 to 1
- phase: float32 [16, 1280], P(('grating', 'layer'), 'harm'), parts along dimension 0, may hold values from -3.140625 to 3.140625
- kept: int32 [16], P(('grating', 'layer')), parts along dimension 0, may hold values from 640 to 1280
- start: int32 [8], P(('grating', 'layer')), parts along dimension 0, may hold values from 0 to 1
Outputs:
- advanced: float32 [8, 1280, 2, 640], P(('grating', 'layer'), 'harm'), parts along dimension 0
The draws below stay inside these ranges and needn't reach their ends.
There are 2 independent parts, one for each index of `grating`. The reference program is written for one: setup_inputs(seed, part) draws one part's arguments, and reference() takes and returns one part's arrays. A program takes and returns all parts, laid end to end along the dimension named above; each array names one. Nothing has to cross between parts.
All inputs are finite; a program needn't handle non-finite values.
Results may differ from the reference program's by a relative error of at most 0.00024.
Values sent between devices are 32-bit elements; how exact they have to be, the bound alone decides.
A program may use at most 128 MiB of HBM per device.

```python
import math
import jax
import jax.numpy as jnp
from jax import lax

HARM = 1280
COLS = 640
LAYER_DEV = 2
LAYERS = 8
PANELS = 4


def with_ends(array, key, smallest, largest):
    shape = array.shape
    place = [jax.random.randint(jax.random.fold_in(key, axis), (), 0, shape[axis]) for axis in range(len(shape))]
    array = array.at[tuple(place)].set(smallest)
    longest = shape.index(max(shape))
    place[longest] = (place[longest] + 1) % shape[longest]
    return array.at[tuple(place)].set(largest)


def shard_levels(own_key, shape, shards, low, high):
    def one(dim, parts):
        heights = jax.random.uniform(jax.random.fold_in(jax.random.fold_in(own_key, 6), dim), (parts,), jnp.float32, low / len(shards), high / len(shards))
        return jnp.repeat(jnp.exp(heights), shape[dim] // parts).reshape((-1,) + (1,) * (len(shape) - dim - 1))

    level = one(*shards[0])
    for cut in shards[1:]:
        level = level * one(*cut)
    return level


def gaussian(rng, extent, scale, bound, split=(), dtype=jnp.bfloat16):
    array = scale * jax.random.normal(rng, extent, jnp.float32)
    if split:
        array = array * shard_levels(rng, extent, split, -0.22, 0.18)
    return jnp.clip(array, -bound, bound).astype(dtype)


def setup_inputs(seed: int = 0, part: int = 0) -> dict:
    arg_keys = jax.random.split(jax.random.key(seed), 7)
    part_keys = jax.random.split(jax.random.fold_in(arg_keys[6], part), 7)
    return {
        "panels": gaussian(part_keys[0], (PANELS, HARM, 2, COLS), 1.0, 6.0, ((0, 4), (1, 4)), jnp.float32),
        "factors": gaussian(part_keys[1], (LAYERS, HARM, 2, HARM), (HARM // 2) ** -0.5, 0.25, ((0, 4), (1, 4)), jnp.float32),
        "decay": jnp.clip(jnp.exp(math.log(1.0) - 1.3862944 * jax.random.uniform(part_keys[2], (LAYERS, HARM), jnp.float32) ** shard_levels(part_keys[2], (LAYERS, HARM), ((0, 4), (1, 4)), -0.2, 0.2)), 0.25, 1.0),
        "phase": jnp.clip(jax.random.uniform(part_keys[3], (LAYERS, HARM), jnp.float32, -3.140625, 3.140625), -3.140625, 3.140625),
        "kept": with_ends(jax.random.randint(part_keys[4], (LAYERS,), HARM // 2, HARM + 1), jax.random.fold_in(part_keys[4], 1), HARM // 2, HARM).astype(jnp.int32),
        "start": with_ends(jax.random.randint(part_keys[5], (PANELS,), 0, LAYER_DEV), jax.random.fold_in(part_keys[5], 1), 0, LAYER_DEV - 1).astype(jnp.int32),
    }


def contract(left_matrix, right_matrix):
    return jnp.dot(left_matrix.T, right_matrix, precision=lax.Precision.HIGHEST, preferred_element_type=jnp.float32)


def reference(panels, factors, decay, phase, kept, start):
    harmonic_index = lax.iota(jnp.int32, HARM)
    finished = []
    for group_id in range(PANELS):
        current = panels[group_id]
        for section_step in range(LAYER_DEV):
            layer_id = (group_id * LAYER_DEV + (start[group_id] + section_step) % LAYER_DEV).astype(jnp.int32)
            factor_block = factors[layer_id]
            live_rows = (harmonic_index < kept[layer_id]).astype(jnp.float32)
            magnitude = decay[layer_id] * live_rows
            prop_real = (magnitude * jnp.cos(phase[layer_id]))[:, None]
            prop_imag = (magnitude * jnp.sin(phase[layer_id]))[:, None]
            real_in = prop_real * current[:, 0] - prop_imag * current[:, 1]
            imag_in = prop_real * current[:, 1] + prop_imag * current[:, 0]
            real_out = contract(factor_block[:, 0], real_in) - contract(factor_block[:, 1], imag_in)
            imag_out = contract(factor_block[:, 0], imag_in) + contract(factor_block[:, 1], real_in)
            current = jnp.stack([real_out, imag_out], 1)
        finished.append(current)
    return jnp.roll(jnp.stack(finished), 1, axis=0)
```

```python
import functools

import jax
import jax.numpy as jnp
from jax import lax
from jax.experimental import pallas as pl
from jax.experimental.layout import Layout, with_layout_constraint
from jax.experimental.pallas import tpu as pltpu
from jax.sharding import PartitionSpec as P

LANES = 128
CORES = 2
MESH = pl.DeviceIdType.MESH


def split(value):
    high = value.astype(jnp.bfloat16)
    low = (value - high.astype(jnp.float32)).astype(jnp.bfloat16)
    return high, low


def kernel(
    steps, chips, groups, rows, harmonics, chunks, depth,
    start_ref, kept_ref, decay_ref, phase_ref, panel_ref, factor_ref, out_ref,
    matrix, right, prop, own, sib_send, sib_recv, keep, far_send, far_recv, next_send,
    sib_ss, sib_rs, far_ss, far_rs, next_ss, next_rs,
):
    harm = lax.axis_index("harm")
    layer = lax.axis_index("layer")
    chip, core = harm // CORES, lax.rem(harm, CORES)
    other = 1 - core
    sibling = {"harm": chip * CORES + other}
    after = {"layer": lax.rem(layer + 1, groups)}
    before = {"layer": lax.rem(layer + groups - 1, groups)}
    width = 2 * LANES
    tiles = harmonics // LANES

    def far_chip(distance):
        return lax.rem(chip + distance, chips)

    def far_device(distance):
        return {"harm": far_chip(distance) * CORES + core}

    barrier = pltpu.get_barrier_semaphore()
    friends = [sibling, after, before] + [far_device(d) for d in range(1, chips)]
    for friend in friends:
        pl.semaphore_signal(barrier, inc=1, device_id=friend, device_id_type=MESH)

    def sib_copy(step, q):
        return pltpu.make_async_remote_copy(
            src_ref=sib_send.at[step, q], dst_ref=sib_recv.at[step, q],
            send_sem=sib_ss.at[step, q], recv_sem=sib_rs.at[step, q],
            device_id=sibling, device_id_type=MESH,
        )

    def far_copy(step, q, distance):
        return pltpu.make_async_remote_copy(
            src_ref=far_send.at[step, q, distance - 1],
            dst_ref=far_recv.at[step, q, distance - 1],
            send_sem=far_ss.at[step, q, distance - 1],
            recv_sem=far_rs.at[step, q, distance - 1],
            device_id=far_device(distance), device_id_type=MESH,
        )

    def next_copy(q):
        return pltpu.make_async_remote_copy(
            src_ref=next_send.at[q], dst_ref=out_ref.at[q],
            send_sem=next_ss.at[q], recv_sem=next_rs.at[q],
            device_id=after, device_id_type=MESH,
        )

    def load_matrix(step):
        base = lax.rem(start_ref[0] + step, steps) * (rows * tiles * 2)

        def one(tile, carry):
            first = base + tile * 2
            real = factor_ref[pl.ds(first, rows, stride=tiles * 2), :]
            imag = factor_ref[pl.ds(first + 1, rows, stride=tiles * 2), :]
            high, low = split(jnp.concatenate([real, imag], 0).T)
            here = pl.ds(pl.multiple_of(tile * LANES, LANES), LANES)
            matrix[step, here, 0:2 * rows] = high
            matrix[step, here, depth:depth + 2 * rows] = high
            matrix[step, here, 2 * depth:2 * depth + 2 * rows] = low
            return carry

        lax.fori_loop(0, tiles, one, 0)

    def propagator(step):
        layer_id = lax.rem(start_ref[0] + step, steps)
        index = harm * rows + lax.broadcasted_iota(jnp.int32, (1, rows), 1)
        live = (index < kept_ref[layer_id]).astype(jnp.float32)
        magnitude = decay_ref[pl.ds(layer_id, 1), :] * live
        angles = phase_ref[pl.ds(layer_id, 1), :]
        for part, line in enumerate((magnitude * jnp.cos(angles), magnitude * jnp.sin(angles))):
            prop[step, part] = jnp.broadcast_to(line, (LANES, rows)).T

    def load_right(step, real, imag):
        prop_real, prop_imag = prop[step, 0], prop[step, 1]
        high_r, low_r = split(prop_real * real - prop_imag * imag)
        high_i, low_i = split(prop_real * imag + prop_imag * real)
        for place, r, i in ((0, high_r, high_i), (depth, low_r, low_i), (2 * depth, high_r, high_i)):
            right[place:place + rows, 0:LANES] = r
            right[place:place + rows, LANES:width] = i
            right[place + rows:place + 2 * rows, 0:LANES] = -i
            right[place + rows:place + 2 * rows, LANES:width] = r

    def block(index):
        return pl.ds(pl.multiple_of(index * rows, rows), rows)

    def product(step, index):
        return jnp.dot(
            matrix[step, block(index), :], right[...], preferred_element_type=jnp.float32
        )

    def contribute(step, q):
        def give(place, carry):
            sib_send[step, q, block(place), :] = product(step, place * CORES + other)
            return carry

        lax.fori_loop(0, chips, give, 0)
        sib_copy(step, q).start()

        def hold(place, carry):
            own[block(place), :] = product(step, place * CORES + core)
            return carry

        lax.fori_loop(0, chips, hold, 0)
        sib_copy(step, q).wait_recv()
        for distance in range(1, chips):
            there = block(far_chip(distance))
            far_send[step, q, distance - 1] = own[there, :] + sib_recv[step, q, there, :]
            far_copy(step, q, distance).start()
        mine = block(chip)
        keep[step, q] = own[mine, :] + sib_recv[step, q, mine, :]

    def collect(step, q):
        total = keep[step, q]
        for distance in range(1, chips):
            far_copy(step, q, distance).wait_recv()
            total = total + far_recv[step, q, distance - 1]
        return total

    if depth > 2 * rows:
        matrix[...] = jnp.zeros_like(matrix)
        right[...] = jnp.zeros_like(right)

    for step in range(steps):
        propagator(step)
    load_matrix(0)
    pl.semaphore_wait(barrier, len(friends))

    def enter(q, carry):
        first = q * 2
        load_right(
            0,
            panel_ref[pl.ds(first, rows, stride=chunks * 2), :],
            panel_ref[pl.ds(first + 1, rows, stride=chunks * 2), :],
        )
        contribute(0, q)
        return carry

    lax.fori_loop(0, chunks, enter, 0)

    for step in range(1, steps):
        load_matrix(step)

        def advance(q, carry, step=step):
            total = collect(step - 1, q)
            load_right(step, total[:, 0:LANES], total[:, LANES:width])
            contribute(step, q)
            return carry

        lax.fori_loop(0, chunks, advance, 0)

    def leave(q, carry):
        next_send[q] = collect(steps - 1, q)
        next_copy(q).start()
        return carry

    lax.fori_loop(0, chunks, leave, 0)

    def finish(q, carry):
        for step in range(steps):
            sib_copy(step, q).wait_send()
            for distance in range(1, chips):
                far_copy(step, q, distance).wait_send()
        next_copy(q).wait()
        return carry

    lax.fori_loop(0, chunks, finish, 0)


def lines(array):
    lead = array.shape[:-1]
    tiles = array.shape[-1] // LANES
    split_up = array.reshape(-1, lead[-1], tiles, LANES)
    split_up = with_layout_constraint(split_up, Layout(major_to_minor=(0, 2, 1, 3)))
    return split_up.transpose(0, 2, 1, 3).reshape(-1, LANES)


def on_device(panels, factors, decay, phase, kept, start):
    steps, rows, _, harmonics = factors.shape
    columns = panels.shape[-1]
    chips = lax.axis_size("harm") // CORES
    groups = lax.axis_size("layer")
    chunks = columns // LANES
    depth = -(-2 * rows // LANES) * LANES
    width = 2 * LANES

    vmem = pl.BlockSpec(memory_space=pltpu.VMEM)
    smem = pl.BlockSpec(memory_space=pltpu.SMEM)
    dma = pltpu.SemaphoreType.DMA
    far = max(chips - 1, 1)
    result = pl.pallas_call(
        functools.partial(kernel, steps, chips, groups, rows, harmonics, chunks, depth),
        out_shape=jax.ShapeDtypeStruct((chunks, rows, width), jnp.float32),
        in_specs=[smem, smem, vmem, vmem, vmem, vmem],
        out_specs=vmem,
        scratch_shapes=[
            pltpu.VMEM((steps, harmonics, 3 * depth), jnp.bfloat16),
            pltpu.VMEM((3 * depth, width), jnp.bfloat16),
            pltpu.VMEM((steps, 2, rows, LANES), jnp.float32),
            pltpu.VMEM((chips * rows, width), jnp.float32),
            pltpu.VMEM((steps, chunks, chips * rows, width), jnp.float32),
            pltpu.VMEM((steps, chunks, chips * rows, width), jnp.float32),
            pltpu.VMEM((steps, chunks, rows, width), jnp.float32),
            pltpu.VMEM((steps, chunks, far, rows, width), jnp.float32),
            pltpu.VMEM((steps, chunks, far, rows, width), jnp.float32),
            pltpu.VMEM((chunks, rows, width), jnp.float32),
            dma((steps, chunks)),
            dma((steps, chunks)),
            dma((steps, chunks, far)),
            dma((steps, chunks, far)),
            dma((chunks,)),
            dma((chunks,)),
        ],
        compiler_params=pltpu.CompilerParams(
            collective_id=0, has_side_effects=True, vmem_limit_bytes=60 * 2**20
        ),
    )(start, kept, decay, phase, lines(panels), lines(factors))
    result = result.reshape(chunks, rows, 2, LANES).transpose(1, 2, 0, 3)
    result = with_layout_constraint(result, Layout(major_to_minor=(0, 2, 1, 3)))
    return result.reshape(panels.shape)


def solution(mesh):
    in_specs = (
        P(("grating", "layer"), "harm", None, None),
        P(("grating", "layer"), "harm", None, None),
        P(("grating", "layer"), "harm"),
        P(("grating", "layer"), "harm"),
        P(("grating", "layer")),
        P(("grating", "layer")),
    )
    out_specs = P(("grating", "layer"), "harm", None, None)
    return jax.shard_map(
        on_device, mesh=mesh, in_specs=in_specs, out_specs=out_specs, check_vma=False
    )
```

```python
import functools

import jax
import jax.numpy as jnp
from jax import lax
from jax.experimental import pallas as pl
from jax.experimental.layout import Layout, with_layout_constraint
from jax.experimental.pallas import tpu as pltpu
from jax.sharding import PartitionSpec as P

LANES = 128
CORES = 2
MESH = pl.DeviceIdType.MESH


def split(value):
    high = value.astype(jnp.bfloat16)
    low = (value - high.astype(jnp.float32)).astype(jnp.bfloat16)
    return high, low


def kernel(
    steps, chips, groups, rows, harmonics, chunks, depth, pieces,
    start_ref, kept_ref, decay_ref, phase_ref, panel_hbm, factor_hbm, out_hbm,
    panel_ref, factor_ref, out_ref,
    matrix, right, prop, own, sib_send, sib_recv, keep, far_send, far_recv, next_send, next_recv,
    in_sem, out_sem, sib_ss, sib_rs, far_ss, far_rs, next_ss, next_rs,
):
    harm = lax.axis_index("harm")
    layer = lax.axis_index("layer")
    chip, core = harm // CORES, lax.rem(harm, CORES)
    other = 1 - core
    sibling = {"harm": chip * CORES + other}
    after = {"layer": lax.rem(layer + 1, groups)}
    before = {"layer": lax.rem(layer + groups - 1, groups)}
    width = 2 * LANES
    tiles = harmonics // LANES
    piece_rows = rows // pieces
    out_rows = piece_rows * chunks * 2

    def far_chip(distance):
        return lax.rem(chip + distance, chips)

    def far_device(distance):
        return {"harm": far_chip(distance) * CORES + core}

    panel_copy = pltpu.make_async_copy(panel_hbm, panel_ref, in_sem.at[0])
    panel_copy.start()
    share = rows * tiles * 2
    factor_copies = [
        pltpu.make_async_copy(
            factor_hbm.at[pl.ds(part * share, share), :],
            factor_ref.at[pl.ds(part * share, share), :],
            in_sem.at[1 + part],
        )
        for part in range(steps)
    ]
    for copy in factor_copies:
        copy.start()

    barrier = pltpu.get_barrier_semaphore()
    friends = [sibling, after, before] + [far_device(d) for d in range(1, chips)]
    for friend in friends:
        pl.semaphore_signal(barrier, inc=1, device_id=friend, device_id_type=MESH)

    def sib_copy(step, q, distance):
        return pltpu.make_async_remote_copy(
            src_ref=sib_send.at[step, q, distance], dst_ref=sib_recv.at[step, q, distance],
            send_sem=sib_ss.at[step, q, distance], recv_sem=sib_rs.at[step, q, distance],
            device_id=sibling, device_id_type=MESH,
        )

    def strip(piece):
        return pl.ds(piece * piece_rows, piece_rows)

    def far_copy(step, q, distance, piece):
        place = (step, q, distance - 1)
        return pltpu.make_async_remote_copy(
            src_ref=far_send.at[(*place, strip(piece))],
            dst_ref=far_recv.at[(*place, strip(piece))],
            send_sem=far_ss.at[(*place, piece)],
            recv_sem=far_rs.at[(*place, piece)],
            device_id=far_device(distance), device_id_type=MESH,
        )

    def next_copy(q, piece):
        return pltpu.make_async_remote_copy(
            src_ref=next_send.at[q, strip(piece)], dst_ref=next_recv.at[q, strip(piece)],
            send_sem=next_ss.at[q, piece], recv_sem=next_rs.at[q, piece],
            device_id=after, device_id_type=MESH,
        )

    def out_copy(piece):
        here = pl.ds(piece * out_rows, out_rows)
        return pltpu.make_async_copy(out_ref.at[here], out_hbm.at[here], out_sem.at[piece])

    def load_matrix(step, from_tile, count):
        base = lax.rem(start_ref[0] + step, steps) * (rows * tiles * 2)

        def one(turn, carry):
            tile = lax.rem(from_tile + turn, tiles)
            first = base + tile * 2
            real = factor_ref[pl.ds(first, rows, stride=tiles * 2), :]
            imag = factor_ref[pl.ds(first + 1, rows, stride=tiles * 2), :]
            high, low = split(jnp.concatenate([real, imag], 0).T)
            here = pl.ds(pl.multiple_of(tile * LANES, LANES), LANES)
            matrix[step, here, 0:2 * rows] = high
            matrix[step, here, depth:depth + 2 * rows] = high
            matrix[step, here, 2 * depth:2 * depth + 2 * rows] = low
            return carry

        lax.fori_loop(0, count, one, 0)

    def propagator(step):
        layer_id = lax.rem(start_ref[0] + step, steps)
        index = harm * rows + lax.broadcasted_iota(jnp.int32, (1, rows), 1)
        live = (index < kept_ref[layer_id]).astype(jnp.float32)
        magnitude = decay_ref[pl.ds(layer_id, 1), :] * live
        angles = phase_ref[pl.ds(layer_id, 1), :]
        for part, line in enumerate((magnitude * jnp.cos(angles), magnitude * jnp.sin(angles))):
            prop[step, part] = jnp.broadcast_to(line, (LANES, rows)).T

    def load_right(step, real, imag):
        prop_real, prop_imag = prop[step, 0], prop[step, 1]
        high_r, low_r = split(prop_real * real - prop_imag * imag)
        high_i, low_i = split(prop_real * imag + prop_imag * real)
        for place, r, i in ((0, high_r, high_i), (depth, low_r, low_i), (2 * depth, high_r, high_i)):
            right[place:place + rows, 0:LANES] = r
            right[place:place + rows, LANES:width] = i
            right[place + rows:place + 2 * rows, 0:LANES] = -i
            right[place + rows:place + 2 * rows, LANES:width] = r

    def product(step, index):
        here = pl.ds(pl.multiple_of(index * rows, rows), rows)
        return jnp.dot(matrix[step, here, :], right[...], preferred_element_type=jnp.float32)

    def give(step, q, distance):
        sib_send[step, q, distance] = product(step, far_chip(distance) * CORES + other)
        sib_copy(step, q, distance).start()

    def far_products(step, q):
        def one(distance, carry):
            give(step, q, distance)
            own[distance - 1] = product(step, far_chip(distance) * CORES + core)
            return carry

        lax.fori_loop(1, chips, one, 0)

    def far_sums(step, q):
        for distance in range(1, chips):
            sib_copy(step, q, distance).wait_recv()
            far_send[step, q, distance - 1] = own[distance - 1] + sib_recv[step, q, distance]
            for piece in range(pieces):
                far_copy(step, q, distance, piece).start()

    def hold(step, q):
        keep[step, q] = product(step, harm)

    def contribute(step, q):
        far_products(step, q)
        give(step, q, 0)
        far_sums(step, q)
        hold(step, q)

    def load_panel(q):
        first = q * 2
        load_right(
            0,
            panel_ref[pl.ds(first, rows, stride=chunks * 2), :],
            panel_ref[pl.ds(first + 1, rows, stride=chunks * 2), :],
        )

    if depth > 2 * rows:
        matrix[...] = jnp.zeros_like(matrix)
        right[...] = jnp.zeros_like(right)

    for step in range(steps):
        propagator(step)
    panel_copy.wait()
    load_panel(0)
    for copy in factor_copies:
        copy.wait()
    near = CORES * rows // LANES if CORES * rows % LANES == 0 else 0
    load_matrix(0, far_chip(1) * near, tiles - near)
    pl.semaphore_wait(barrier, len(friends))

    far_products(0, 0)
    load_matrix(0, chip * near, near)
    far_sums(0, 0)
    give(0, 0, 0)
    hold(0, 0)

    def enter(q, carry):
        load_panel(q)
        contribute(0, q)
        return carry

    lax.fori_loop(1, chunks, enter, 0)

    for step in range(1, steps):
        load_matrix(step, 0, tiles)

        def advance(q, carry, step=step):
            sib_copy(step - 1, q, 0).wait_recv()
            total = keep[step - 1, q] + sib_recv[step - 1, q, 0]
            for distance in range(1, chips):
                for piece in range(pieces):
                    far_copy(step - 1, q, distance, piece).wait_recv()
                total = total + far_recv[step - 1, q, distance - 1]
            load_right(step, total[:, 0:LANES], total[:, LANES:width])
            contribute(step, q)
            return carry

        lax.fori_loop(0, chunks, advance, 0)

    last = steps - 1

    def leave(q, carry):
        sib_copy(last, q, 0).wait_recv()
        for piece in range(pieces):
            here = strip(piece)
            total = keep[last, q, here] + sib_recv[last, q, 0, here]
            for distance in range(1, chips):
                far_copy(last, q, distance, piece).wait_recv()
                total = total + far_recv[last, q, distance - 1, here]
            next_send[q, here] = total
            next_copy(q, piece).start()
        return carry

    lax.fori_loop(0, chunks, leave, 0)

    for q in range(chunks):
        for piece in range(pieces):
            next_copy(q, piece).wait_recv()
            for part in range(2):
                there = pl.ds(piece * out_rows + q * 2 + part, piece_rows, stride=chunks * 2)
                out_ref[there, :] = next_recv[q, strip(piece), part * LANES:(part + 1) * LANES]
            if q == chunks - 1:
                out_copy(piece).start()

    def finish(q, carry):
        for step in range(steps):
            for distance in range(chips):
                sib_copy(step, q, distance).wait_send()
            for distance in range(1, chips):
                for piece in range(pieces):
                    far_copy(step, q, distance, piece).wait_send()
        for piece in range(pieces):
            next_copy(q, piece).wait_send()
        return carry

    lax.fori_loop(0, chunks, finish, 0)
    for piece in range(pieces):
        out_copy(piece).wait()


def lines(array):
    lead = array.shape[:-1]
    tiles = array.shape[-1] // LANES
    split_up = array.reshape(-1, lead[-1], tiles, LANES)
    split_up = with_layout_constraint(split_up, Layout(major_to_minor=(0, 2, 1, 3)))
    return split_up.transpose(0, 2, 1, 3).reshape(-1, LANES)


def on_device(panels, factors, decay, phase, kept, start):
    steps, rows, _, harmonics = factors.shape
    columns = panels.shape[-1]
    chips = lax.axis_size("harm") // CORES
    groups = lax.axis_size("layer")
    chunks = columns // LANES
    depth = -(-2 * rows // LANES) * LANES
    width = 2 * LANES

    pieces = next(count for count in (5, 4, 2, 1) if rows % (8 * count) == 0)
    vmem = pl.BlockSpec(memory_space=pltpu.VMEM)
    smem = pl.BlockSpec(memory_space=pltpu.SMEM)
    hbm = pl.BlockSpec(memory_space=pl.ANY)
    dma = pltpu.SemaphoreType.DMA
    far = max(chips - 1, 1)
    panel_lines, factor_lines = lines(panels), lines(factors)
    result = pl.pallas_call(
        functools.partial(kernel, steps, chips, groups, rows, harmonics, chunks, depth, pieces),
        out_shape=jax.ShapeDtypeStruct(panel_lines.shape, jnp.float32),
        in_specs=[smem, smem, vmem, vmem, hbm, hbm],
        out_specs=hbm,
        scratch_shapes=[
            pltpu.VMEM(panel_lines.shape, jnp.float32),
            pltpu.VMEM(factor_lines.shape, jnp.float32),
            pltpu.VMEM(panel_lines.shape, jnp.float32),
            pltpu.VMEM((steps, harmonics, 3 * depth), jnp.bfloat16),
            pltpu.VMEM((3 * depth, width), jnp.bfloat16),
            pltpu.VMEM((steps, 2, rows, LANES), jnp.float32),
            pltpu.VMEM((far, rows, width), jnp.float32),
            pltpu.VMEM((steps, chunks, chips, rows, width), jnp.float32),
            pltpu.VMEM((steps, chunks, chips, rows, width), jnp.float32),
            pltpu.VMEM((steps, chunks, rows, width), jnp.float32),
            pltpu.VMEM((steps, chunks, far, rows, width), jnp.float32),
            pltpu.VMEM((steps, chunks, far, rows, width), jnp.float32),
            pltpu.VMEM((chunks, rows, width), jnp.float32),
            pltpu.VMEM((chunks, rows, width), jnp.float32),
            dma((1 + steps,)),
            dma((pieces,)),
            dma((steps, chunks, chips)),
            dma((steps, chunks, chips)),
            dma((steps, chunks, far, pieces)),
            dma((steps, chunks, far, pieces)),
            dma((chunks, pieces)),
            dma((chunks, pieces)),
        ],
        compiler_params=pltpu.CompilerParams(
            collective_id=0, has_side_effects=True, vmem_limit_bytes=60 * 2**20
        ),
    )(start, kept, decay, phase, panel_lines, factor_lines)
    result = result.reshape(rows, chunks, 2, LANES).transpose(0, 2, 1, 3)
    result = with_layout_constraint(result, Layout(major_to_minor=(0, 2, 1, 3)))
    return result.reshape(panels.shape)


def solution(mesh):
    in_specs = (
        P(("grating", "layer"), "harm", None, None),
        P(("grating", "layer"), "harm", None, None),
        P(("grating", "layer"), "harm"),
        P(("grating", "layer"), "harm"),
        P(("grating", "layer")),
        P(("grating", "layer")),
    )
    out_specs = P(("grating", "layer"), "harm", None, None)
    return jax.shard_map(
        on_device, mesh=mesh, in_specs=in_specs, out_specs=out_specs, check_vma=False
    )
```

```python
import functools

import jax
import jax.numpy as jnp
from jax import lax
from jax.experimental import pallas as pl
from jax.experimental.layout import Layout, with_layout_constraint
from jax.experimental.pallas import tpu as pltpu
from jax.sharding import PartitionSpec as P

LANES = 128
CORES = 2
MESH = pl.DeviceIdType.MESH


def split(value):
    high = value.astype(jnp.bfloat16)
    low = (value - high.astype(jnp.float32)).astype(jnp.bfloat16)
    return high, low


def kernel(
    steps, chips, groups, rows, harmonics, chunks, depth, pieces,
    start_ref, kept_ref, decay_ref, phase_ref, panel_hbm, factor_hbm, out_hbm,
    panel_ref, factor_ref, out_ref,
    matrix, right, prop, own, sib_send, sib_recv, keep, far_send, far_recv, next_send, next_recv,
    in_sem, out_sem, sib_ss, sib_rs, far_ss, far_rs, next_ss, next_rs,
):
    harm = lax.axis_index("harm")
    layer = lax.axis_index("layer")
    chip, core = harm // CORES, lax.rem(harm, CORES)
    other = 1 - core
    sibling = {"harm": chip * CORES + other}
    after = {"layer": lax.rem(layer + 1, groups)}
    before = {"layer": lax.rem(layer + groups - 1, groups)}
    width = 2 * LANES
    tiles = harmonics // LANES
    piece_rows = rows // pieces
    out_rows = piece_rows * chunks * 2

    def far_chip(distance):
        return lax.rem(chip + distance, chips)

    def far_device(distance):
        return {"harm": far_chip(distance) * CORES + core}

    panel_copy = pltpu.make_async_copy(panel_hbm, panel_ref, in_sem.at[0])
    panel_copy.start()
    share = rows * tiles * 2
    factor_copies = [
        pltpu.make_async_copy(
            factor_hbm.at[pl.ds(part * share, share), :],
            factor_ref.at[pl.ds(part * share, share), :],
            in_sem.at[1 + part],
        )
        for part in range(steps)
    ]
    for copy in factor_copies:
        copy.start()

    barrier = pltpu.get_barrier_semaphore()
    friends = [sibling, after, before] + [far_device(d) for d in range(1, chips)]
    for friend in friends:
        pl.semaphore_signal(barrier, inc=1, device_id=friend, device_id_type=MESH)

    def sib_copy(step, q, distance):
        return pltpu.make_async_remote_copy(
            src_ref=sib_send.at[step, q, distance], dst_ref=sib_recv.at[step, q, distance],
            send_sem=sib_ss.at[step, q, distance], recv_sem=sib_rs.at[step, q, distance],
            device_id=sibling, device_id_type=MESH,
        )

    def cuts(step):
        return pieces if step == steps - 1 else 1

    def strip(piece, count=pieces):
        return pl.ds(piece * (rows // count), rows // count)

    def far_copy(step, q, distance, piece):
        place = (step, q, distance - 1)
        return pltpu.make_async_remote_copy(
            src_ref=far_send.at[(*place, strip(piece, cuts(step)))],
            dst_ref=far_recv.at[(*place, strip(piece, cuts(step)))],
            send_sem=far_ss.at[(*place, piece)],
            recv_sem=far_rs.at[(*place, piece)],
            device_id=far_device(distance), device_id_type=MESH,
        )

    def next_copy(q, piece):
        return pltpu.make_async_remote_copy(
            src_ref=next_send.at[q, strip(piece)], dst_ref=next_recv.at[q, strip(piece)],
            send_sem=next_ss.at[q, piece], recv_sem=next_rs.at[q, piece],
            device_id=after, device_id_type=MESH,
        )

    def out_copy(piece):
        here = pl.ds(piece * out_rows, out_rows)
        return pltpu.make_async_copy(out_ref.at[here], out_hbm.at[here], out_sem.at[piece])

    def load_matrix(step, from_tile, count):
        base = lax.rem(start_ref[0] + step, steps) * (rows * tiles * 2)

        def one(turn, carry):
            tile = lax.rem(from_tile + turn, tiles)
            first = base + tile * 2
            real = factor_ref[pl.ds(first, rows, stride=tiles * 2), :]
            imag = factor_ref[pl.ds(first + 1, rows, stride=tiles * 2), :]
            high, low = split(jnp.concatenate([real, imag], 0).T)
            here = pl.ds(pl.multiple_of(tile * LANES, LANES), LANES)
            matrix[step, here, 0:2 * rows] = high
            matrix[step, here, depth:depth + 2 * rows] = high
            matrix[step, here, 2 * depth:2 * depth + 2 * rows] = low
            return carry

        lax.fori_loop(0, count, one, 0)

    def propagator(step):
        layer_id = lax.rem(start_ref[0] + step, steps)
        index = harm * rows + lax.broadcasted_iota(jnp.int32, (1, rows), 1)
        live = (index < kept_ref[layer_id]).astype(jnp.float32)
        magnitude = decay_ref[pl.ds(layer_id, 1), :] * live
        angles = phase_ref[pl.ds(layer_id, 1), :]
        for part, line in enumerate((magnitude * jnp.cos(angles), magnitude * jnp.sin(angles))):
            prop[step, part] = jnp.broadcast_to(line, (LANES, rows)).T

    def load_right(step, real, imag):
        prop_real, prop_imag = prop[step, 0], prop[step, 1]
        high_r, low_r = split(prop_real * real - prop_imag * imag)
        high_i, low_i = split(prop_real * imag + prop_imag * real)
        for place, r, i in ((0, high_r, high_i), (depth, low_r, low_i), (2 * depth, high_r, high_i)):
            right[place:place + rows, 0:LANES] = r
            right[place:place + rows, LANES:width] = i
            right[place + rows:place + 2 * rows, 0:LANES] = -i
            right[place + rows:place + 2 * rows, LANES:width] = r

    def product(step, index):
        here = pl.ds(pl.multiple_of(index * rows, rows), rows)
        return jnp.dot(matrix[step, here, :], right[...], preferred_element_type=jnp.float32)

    def give(step, q, distance):
        sib_send[step, q, distance] = product(step, far_chip(distance) * CORES + other)
        sib_copy(step, q, distance).start()

    def far_products(step, q):
        def one(distance, carry):
            give(step, q, distance)
            own[distance - 1] = product(step, far_chip(distance) * CORES + core)
            return carry

        lax.fori_loop(1, chips, one, 0)

    def far_sums(step, q):
        for distance in range(1, chips):
            sib_copy(step, q, distance).wait_recv()
            for piece in range(cuts(step)):
                here = strip(piece, cuts(step))
                far_send[step, q, distance - 1, here] = (
                    own[distance - 1, here] + sib_recv[step, q, distance, here]
                )
                far_copy(step, q, distance, piece).start()

    def hold(step, q):
        keep[step, q] = product(step, harm)

    def contribute(step, q):
        far_products(step, q)
        give(step, q, 0)
        far_sums(step, q)
        hold(step, q)

    def load_panel(q):
        first = q * 2
        load_right(
            0,
            panel_ref[pl.ds(first, rows, stride=chunks * 2), :],
            panel_ref[pl.ds(first + 1, rows, stride=chunks * 2), :],
        )

    if depth > 2 * rows:
        matrix[...] = jnp.zeros_like(matrix)
        right[...] = jnp.zeros_like(right)

    for step in range(steps):
        propagator(step)
    panel_copy.wait()
    load_panel(0)
    for copy in factor_copies:
        copy.wait()
    near = CORES * rows // LANES if CORES * rows % LANES == 0 else 0
    load_matrix(0, far_chip(1) * near, tiles - near)
    pl.semaphore_wait(barrier, len(friends))

    far_products(0, 0)
    far_sums(0, 0)
    load_matrix(0, chip * near, near)
    give(0, 0, 0)
    hold(0, 0)

    def enter(q, carry):
        load_panel(q)
        contribute(0, q)
        return carry

    lax.fori_loop(1, chunks, enter, 0)

    for step in range(1, steps):
        load_matrix(step, 0, tiles)

        def advance(q, carry, step=step):
            sib_copy(step - 1, q, 0).wait_recv()
            total = keep[step - 1, q] + sib_recv[step - 1, q, 0]
            for distance in range(1, chips):
                for piece in range(cuts(step - 1)):
                    far_copy(step - 1, q, distance, piece).wait_recv()
                total = total + far_recv[step - 1, q, distance - 1]
            load_right(step, total[:, 0:LANES], total[:, LANES:width])
            contribute(step, q)
            return carry

        lax.fori_loop(0, chunks, advance, 0)

    last = steps - 1

    def leave(q, carry):
        sib_copy(last, q, 0).wait_recv()
        for piece in range(pieces):
            here = strip(piece)
            total = keep[last, q, here] + sib_recv[last, q, 0, here]
            for distance in range(1, chips):
                far_copy(last, q, distance, piece).wait_recv()
                total = total + far_recv[last, q, distance - 1, here]
            next_send[q, here] = total
            next_copy(q, piece).start()
        return carry

    lax.fori_loop(0, chunks, leave, 0)

    for q in range(chunks):
        for piece in range(pieces):
            next_copy(q, piece).wait_recv()
            for part in range(2):
                there = pl.ds(piece * out_rows + q * 2 + part, piece_rows, stride=chunks * 2)
                out_ref[there, :] = next_recv[q, strip(piece), part * LANES:(part + 1) * LANES]
            if q == chunks - 1:
                out_copy(piece).start()

    def finish(q, carry):
        for step in range(steps):
            for distance in range(chips):
                sib_copy(step, q, distance).wait_send()
            for distance in range(1, chips):
                for piece in range(cuts(step)):
                    far_copy(step, q, distance, piece).wait_send()
        for piece in range(pieces):
            next_copy(q, piece).wait_send()
        return carry

    lax.fori_loop(0, chunks, finish, 0)
    for piece in range(pieces):
        out_copy(piece).wait()


def lines(array):
    lead = array.shape[:-1]
    tiles = array.shape[-1] // LANES
    split_up = array.reshape(-1, lead[-1], tiles, LANES)
    split_up = with_layout_constraint(split_up, Layout(major_to_minor=(0, 2, 1, 3)))
    return split_up.transpose(0, 2, 1, 3).reshape(-1, LANES)


def on_device(panels, factors, decay, phase, kept, start):
    steps, rows, _, harmonics = factors.shape
    columns = panels.shape[-1]
    chips = lax.axis_size("harm") // CORES
    groups = lax.axis_size("layer")
    chunks = columns // LANES
    depth = -(-2 * rows // LANES) * LANES
    width = 2 * LANES

    pieces = next(count for count in (2, 1) if rows % (8 * count) == 0)
    vmem = pl.BlockSpec(memory_space=pltpu.VMEM)
    smem = pl.BlockSpec(memory_space=pltpu.SMEM)
    hbm = pl.BlockSpec(memory_space=pl.ANY)
    dma = pltpu.SemaphoreType.DMA
    far = max(chips - 1, 1)
    panel_lines, factor_lines = lines(panels), lines(factors)
    result = pl.pallas_call(
        functools.partial(kernel, steps, chips, groups, rows, harmonics, chunks, depth, pieces),
        out_shape=jax.ShapeDtypeStruct(panel_lines.shape, jnp.float32),
        in_specs=[smem, smem, vmem, vmem, hbm, hbm],
        out_specs=hbm,
        scratch_shapes=[
            pltpu.VMEM(panel_lines.shape, jnp.float32),
            pltpu.VMEM(factor_lines.shape, jnp.float32),
            pltpu.VMEM(panel_lines.shape, jnp.float32),
            pltpu.VMEM((steps, harmonics, 3 * depth), jnp.bfloat16),
            pltpu.VMEM((3 * depth, width), jnp.bfloat16),
            pltpu.VMEM((steps, 2, rows, LANES), jnp.float32),
            pltpu.VMEM((far, rows, width), jnp.float32),
            pltpu.VMEM((steps, chunks, chips, rows, width), jnp.float32),
            pltpu.VMEM((steps, chunks, chips, rows, width), jnp.float32),
            pltpu.VMEM((steps, chunks, rows, width), jnp.float32),
            pltpu.VMEM((steps, chunks, far, rows, width), jnp.float32),
            pltpu.VMEM((steps, chunks, far, rows, width), jnp.float32),
            pltpu.VMEM((chunks, rows, width), jnp.float32),
            pltpu.VMEM((chunks, rows, width), jnp.float32),
            dma((1 + steps,)),
            dma((pieces,)),
            dma((steps, chunks, chips)),
            dma((steps, chunks, chips)),
            dma((steps, chunks, far, pieces)),
            dma((steps, chunks, far, pieces)),
            dma((chunks, pieces)),
            dma((chunks, pieces)),
        ],
        compiler_params=pltpu.CompilerParams(
            collective_id=0, has_side_effects=True, vmem_limit_bytes=60 * 2**20
        ),
    )(start, kept, decay, phase, panel_lines, factor_lines)
    result = result.reshape(rows, chunks, 2, LANES).transpose(0, 2, 1, 3)
    result = with_layout_constraint(result, Layout(major_to_minor=(0, 2, 1, 3)))
    return result.reshape(panels.shape)


def solution(mesh):
    in_specs = (
        P(("grating", "layer"), "harm", None, None),
        P(("grating", "layer"), "harm", None, None),
        P(("grating", "layer"), "harm"),
        P(("grating", "layer"), "harm"),
        P(("grating", "layer")),
        P(("grating", "layer")),
    )
    out_specs = P(("grating", "layer"), "harm", None, None)
    return jax.shard_map(
        on_device, mesh=mesh, in_specs=in_specs, out_specs=out_specs, check_vma=False
    )
```
